32 devices in a mesh: shard: 8 (over z, y), tensor: 4 (over x, core).
Axes of the slice: x: 2, y: 2, z: 4, core: 2. Of those that a mesh axis runs over, the one named last changes fastest.
Arguments:
- grad: float32 [2, 1024, 1024], P(None, 'shard', 'tensor')
- weights: float32 [2, 1024, 1024], P(None, 'shard', 'tensor'), may hold values from -0.1875 to 0.1875
- moment: float32 [4, 8, 256, 256], P('tensor', 'shard'), may hold values from -6 to 6
- second: float32 [4, 8, 256, 256], P('tensor', 'shard'), may hold values from 0.05 to 1
- left_basis: float32 [4, 8, 256, 256], P('tensor', 'shard'), may hold values from -0.375 to 0.375
- right_basis: float32 [4, 8, 256, 256], P('tensor', 'shard'), may hold values from -0.375 to 0.375
- left_gram: float32 [4, 8, 256, 256], P('tensor', 'shard'), as said below
- right_gram: float32 [4, 8, 256, 256], P('tensor', 'shard'), as said below
Outputs:
- new_weights: float32 [2, 1024, 1024], P(None, 'shard', 'tensor')
- moment_out: float32 [4, 8, 256, 256], P('tensor', 'shard')
- second_out: float32 [4, 8, 256, 256], P('tensor', 'shard')
- left_basis_out: float32 [4, 8, 256, 256], P('tensor', 'shard')
- right_basis_out: float32 [4, 8, 256, 256], P('tensor', 'shard')
- left_gram_out: float32 [4, 8, 256, 256], P('tensor', 'shard')
- right_gram_out: float32 [4, 8, 256, 256], P('tensor', 'shard')
The draws below stay inside these ranges and needn't reach their ends.
Inputs may be any that keep to these rules, and one draw needn't show every extreme that they name: `left_gram`: each block is symmetric. `right_gram`: each block is symmetric.
All inputs are finite; a program needn't handle non-finite values.
Results may differ from the reference program's by a relative error of at most 0.0001.
Values sent between devices are 32-bit elements; how exact they have to be, the bound alone decides.
A program may use at most 64 MiB of HBM per device.

```python
import math
import jax
import jax.numpy as jnp
from jax import lax

D = 1024
BLOCK = 256
NS_ITERS = 5
NMAT = 2
CB = 4
NBR = 8
RDEV = 128
RPIECE = 32
N_SHARD = 8


def gram_draw(key):
    shape = (D // BLOCK, NMAT * (D // BLOCK), BLOCK, BLOCK)
    first, later = jax.random.split(key)
    noise = 2.0 * jax.random.normal(first, shape, jnp.float32)
    sym = 0.5 * (noise + jnp.swapaxes(noise, 2, 3))
    level = jax.random.uniform(later, shape[:3], jnp.float32, math.log(16.0), math.log(160.0))
    return sym + jnp.exp(level)[..., None] * jnp.eye(BLOCK, dtype=jnp.float32)


def draw_left_gram(key, part):
    return gram_draw(jax.random.fold_in(key, 11))


def draw_right_gram(key, part):
    return gram_draw(jax.random.fold_in(key, 23))


def draw_grad(key, part):
    shape = (NMAT, D, D)
    first, second_key, third = jax.random.split(key, 3)
    noise = jax.random.normal(first, shape, jnp.float32)
    rise = math.log(3.0)
    row_level = jax.random.uniform(second_key, (NMAT, D, 1), jnp.float32, 0.0, math.log(10.0))
    col_level = jax.random.uniform(third, (NMAT, 1, D), jnp.float32, 0.0, math.log(10.0))
    position = jnp.arange(D, dtype=jnp.float32).reshape(1, D, 1) / (D - 1)
    matrix_index = jnp.arange(NMAT, dtype=jnp.int32).reshape(NMAT, 1, 1)
    row_index = jnp.arange(D, dtype=jnp.int32).reshape(1, D, 1)
    owner = matrix_index * CB + row_index % RDEV // RPIECE
    owner_pos = owner.astype(jnp.float32) / (NBR - 1)
    return noise * jnp.exp(row_level + col_level + rise * position + rise * owner_pos)


def steps_of(rng, extent, pieces, low, top_value):
    gain = 1.0
    for axis_at, blocks in pieces:
        heights = jax.random.uniform(jax.random.fold_in(jax.random.fold_in(rng, 6), axis_at), (blocks,), jnp.float32, low / len(pieces), top_value / len(pieces))
        gain = gain * jnp.repeat(jnp.exp(heights), extent[axis_at] // blocks).reshape((-1,) + (1,) * (len(extent) - 1 - axis_at))
    return gain


def normal_values(rng, extent, scale, reach, pieces=(), kind=jnp.bfloat16):
    values = scale * jax.random.normal(rng, extent, jnp.float32)
    if pieces:
        values = values * steps_of(rng, extent, pieces, -0.22, 0.18)
    return jnp.clip(values, -reach, reach).astype(kind)


def setup_inputs(seed: int = 0) -> dict:
    arg_keys = jax.random.split(jax.random.key(seed), 9)
    grad = draw_grad(jax.random.fold_in(arg_keys[8], 71), 0)
    weights = normal_values(arg_keys[1], (NMAT, D, D), D ** -0.5, 0.1875, ((1, 8), (2, 4)), jnp.float32)
    moment = normal_values(arg_keys[2], (CB, NBR, BLOCK, BLOCK), 0.5, 6.0, ((0, 4), (1, 8)), jnp.float32)
    second = jnp.clip(jnp.exp(math.log(1.0) - 2.9957323 * jax.random.uniform(arg_keys[3], (CB, NBR, BLOCK, BLOCK), jnp.float32) ** steps_of(arg_keys[3], (CB, NBR, BLOCK, BLOCK), ((0, 4), (1, 8)), -0.2, 0.2)), 0.05, 1.0)
    left_basis = normal_values(arg_keys[4], (CB, NBR, BLOCK, BLOCK), BLOCK ** -0.5, 0.375, ((0, 4), (1, 8)), jnp.float32)
    right_basis = normal_values(arg_keys[5], (CB, NBR, BLOCK, BLOCK), BLOCK ** -0.5, 0.375, ((0, 4), (1, 8)), jnp.float32)
    left_gram = draw_left_gram(jax.random.fold_in(arg_keys[8], 71), 0)
    right_gram = draw_right_gram(jax.random.fold_in(arg_keys[8], 71), 0)
    return {"grad": grad, "weights": weights, "moment": moment, "second": second, "left_basis": left_basis, "right_basis": right_basis, "left_gram": left_gram, "right_gram": right_gram}


def to_blocks(full):
    parts = full.reshape(NMAT, N_SHARD, D // BLOCK, BLOCK // N_SHARD, D // BLOCK, BLOCK)
    parts = parts.transpose(4, 0, 2, 1, 3, 5)
    return parts.reshape(D // BLOCK, NMAT * (D // BLOCK), BLOCK, BLOCK)

def from_blocks(blocked):
    parts = blocked.reshape(D // BLOCK, NMAT, D // BLOCK, N_SHARD, BLOCK // N_SHARD, BLOCK)
    parts = parts.transpose(1, 3, 2, 4, 0, 5)
    return parts.reshape(NMAT, D, D)

def matmul_nn(left, right):
    return jnp.einsum('abij,abjk->abik', left, right, precision=lax.Precision.HIGHEST)

def matmul_tn(left, right):
    return jnp.einsum('abji,abjk->abik', left, right, precision=lax.Precision.HIGHEST)

def matmul_nt(left, right):
    return jnp.einsum('abij,abkj->abik', left, right, precision=lax.Precision.HIGHEST)

def refresh(gram, basis):
    power = matmul_nn(gram, basis)
    frob = jnp.sqrt(lax.optimization_barrier(jnp.sum(power * power, axis=(2, 3), keepdims=True)))
    iterate = power / (frob + 1e-06)
    for step in range(NS_ITERS):
        iterate = 1.5 * iterate - 0.5 * matmul_nn(iterate, matmul_tn(iterate, iterate))
    return iterate

def reference(grad, weights, moment, second, left_basis, right_basis, left_gram, right_gram):
    total = jnp.sum(grad * grad)
    limit = 0.5 * jnp.sqrt(jnp.float32(NMAT * D * D))
    scale = jnp.minimum(jnp.float32(1.0), limit / (jnp.sqrt(total) + 1e-06))
    scaled = scale * to_blocks(grad)
    rotated = matmul_tn(left_basis, matmul_nn(scaled, right_basis))
    moment_out = 0.9 * moment + 0.1 * rotated
    second_out = 0.95 * second + 0.05 * rotated * rotated
    normalized = moment_out / (jnp.sqrt(second_out) + 1e-08)
    update = matmul_nt(matmul_nn(left_basis, normalized), right_basis)
    new_weights = weights - 0.03 * (from_blocks(update) + 0.1 * weights)
    left_gram_out = 0.9 * left_gram + 0.1 * matmul_nt(scaled, scaled)
    right_gram_out = 0.9 * right_gram + 0.1 * matmul_tn(scaled, scaled)
    left_basis_out = refresh(left_gram, left_basis)
    right_basis_out = refresh(right_gram, right_basis)
    return (new_weights, moment_out, second_out, left_basis_out, right_basis_out, left_gram_out, right_gram_out)
```

```python
import functools

import jax
import jax.numpy as jnp
from jax import lax
from jax.experimental import pallas as pl
from jax.experimental.pallas import tpu as pltpu
from jax.sharding import PartitionSpec as P

NS_ITERS = 5


learn_rate = 0.03
weight_decay = 0.1

MESH = pl.DeviceIdType.MESH
F32 = jnp.float32
BF16 = jnp.bfloat16


def split(x):
    hi = x.astype(BF16)
    lo = (x - hi.astype(F32)).astype(BF16)
    return hi, lo


def nn(a, b):
    left = jnp.concatenate([a[0], a[1], a[0]], axis=1)
    right = jnp.concatenate([b[0], b[0], b[1]], axis=0)
    return jnp.dot(left, right, preferred_element_type=F32)


def nt(a, b):
    left = jnp.concatenate([a[0], a[1], a[0]], axis=1)
    right = jnp.concatenate([b[0], b[0], b[1]], axis=1)
    return lax.dot_general(left, right, (((1,), (1,)), ((), ())), preferred_element_type=F32)


GRAD_ORDER = (
    (1, 2, 3, 4, 5, 6, 7),
    (2, 3, 4, 5, 6, 7, 0),
    (3, 4, 5, 6, 7, 0, 1),
    (4, 5, 6, 7, 0, 1, 2),
    (5, 6, 7, 0, 1, 2, 3),
    (6, 7, 0, 1, 2, 3, 4),
    (7, 0, 1, 2, 3, 4, 5),
    (0, 1, 2, 3, 4, 5, 6),
)
UPDATE_ORDER = (
    (1, 2, 3, 4, 5, 6, 7),
    (0, 2, 3, 4, 5, 6, 7),
    (0, 1, 3, 4, 5, 6, 7),
    (0, 1, 2, 4, 5, 6, 7),
    (0, 1, 2, 3, 5, 6, 7),
    (0, 1, 2, 3, 4, 6, 7),
    (0, 1, 2, 3, 4, 5, 7),
    (0, 1, 2, 3, 4, 5, 6),
)

SUM_ORDER = (
    (7, 6, 5, 4, 3, 2, 1),
    (7, 6, 5, 4, 3, 2, 0),
    (7, 6, 5, 4, 3, 1, 0),
    (7, 6, 5, 4, 2, 1, 0),
    (0, 1, 2, 3, 5, 6, 7),
    (0, 1, 2, 3, 4, 6, 7),
    (0, 1, 2, 3, 4, 5, 7),
    (0, 1, 2, 3, 4, 5, 6),
)

def peer_table(order, me):
    bit0, bit1, bit2 = lax.rem(me, 2), lax.rem(lax.div(me, 2), 2), lax.div(me, 4)
    place = (1 + 7 * bit0) * (1 + 63 * bit1) * (1 + 4095 * bit2)
    packed = [sum(row[j] * 8 ** i for i, row in enumerate(order)) for j in range(len(order) - 1)]
    return [lax.rem(lax.div(jnp.int32(p), place), 8) for p in packed]


def step_kernel(
    shards, tensors, limit,
    grad, weights, moment, second, left_basis, right_basis, left_gram, right_gram,
    weights_out, moment_out, second_out, left_out, right_out, left_gram_out, right_gram_out,
    grad_own, weights_v, moment_v, second_v, left_v, right_v, left_gram_v, right_gram_v,
    grad_block, update_send, update_recv, part, part_all,
    load_sem, grad_send_sem, grad_recv_sem, up_send_sem, up_recv_sem,
    sum_send_sem, sum_recv_sem, all_send_sem, all_recv_sem,
):
    block = left_v.shape[-1]
    me = lax.axis_index("shard")
    col = lax.axis_index("tensor")
    order = list(range(1, shards))
    grad_peers = peer_table(GRAD_ORDER, me)
    update_peers = peer_table(UPDATE_ORDER, me)

    rows_piece = block // shards

    def left_rows(party):
        starts = [pl.multiple_of(i * rows_piece, rows_piece) for i in party]
        return jnp.concatenate([left_v[pl.ds(start, rows_piece), :] for start in starts], axis=0)

    def shard_peer(k):
        return lax.rem(me + k, shards)

    def tensor_peer(k):
        return lax.rem(col + k, tensors)

    barrier = pltpu.get_barrier_semaphore()
    for k in order:
        pl.semaphore_signal(barrier, inc=1, device_id=(shard_peer(k), col), device_id_type=MESH)
    for k in range(1, tensors):
        pl.semaphore_signal(barrier, inc=1, device_id=(me, tensor_peer(k)), device_id_type=MESH)

    loads = [
        pltpu.make_async_copy(src, dst, load_sem.at[i])
        for i, (src, dst) in enumerate((
            (grad, grad_own),
            (left_gram, left_gram_v),
            (left_basis, left_v),
            (right_gram, right_gram_v),
            (right_basis, right_v),
            (moment, moment_v),
            (second, second_v),
            (weights, weights_v),
        ))
    ]
    for copy in loads:
        copy.start()

    loads[0].wait()
    own = grad_own[...].reshape(block, block)
    squares = jnp.sum((own * own).reshape(block // 8, 8, block), axis=0)
    tile = squares[:, :128]
    for start in range(128, block, 128):
        tile = tile + squares[:, start:start + 128]
    tile = jnp.sum(tile, axis=0, keepdims=True)
    part[me] = tile

    pl.semaphore_wait(barrier, shards - 1 + tensors - 1)

    def grad_copy(peer):
        return pltpu.make_async_remote_copy(
            src_ref=grad_own.at[peer], dst_ref=grad_block.at[me],
            send_sem=grad_send_sem.at[peer], recv_sem=grad_recv_sem.at[me],
            device_id=(peer, col), device_id_type=MESH,
        )

    def sum_copy(peer):
        return pltpu.make_async_remote_copy(
            src_ref=part.at[me], dst_ref=part.at[me],
            send_sem=sum_send_sem.at[peer], recv_sem=sum_recv_sem.at[me],
            device_id=(peer, col), device_id_type=MESH,
        )

    def all_copy(k):
        return pltpu.make_async_remote_copy(
            src_ref=part_all.at[col], dst_ref=part_all.at[col],
            send_sem=all_send_sem.at[k - 1], recv_sem=all_recv_sem.at[k - 1],
            device_id=(me, tensor_peer(k)), device_id_type=MESH,
        )

    def up_copy(peer):
        return pltpu.make_async_remote_copy(
            src_ref=update_send.at[peer], dst_ref=update_recv.at[me],
            send_sem=up_send_sem.at[peer], recv_sem=up_recv_sem.at[me],
            device_id=(peer, col), device_id_type=MESH,
        )

    def landing(buffer, send, recv, source):
        return pltpu.make_async_remote_copy(
            src_ref=buffer.at[source], dst_ref=buffer.at[source],
            send_sem=send.at[source], recv_sem=recv.at[source],
            device_id=(source, col), device_id_type=MESH,
        )

    sum_copies = [sum_copy(p) for p in peer_table(SUM_ORDER, me)]
    grad_copies = [grad_copy(p) for p in grad_peers]
    for copy in sum_copies:
        copy.start()
    for copy in grad_copies:
        copy.start()
    grad_block[me] = grad_own[me]

    for copy in loads[1:5]:
        copy.wait()
    sides = ((left_gram_v, left_v, left_out), (right_gram_v, right_v, right_out))
    for gram, basis, out in sides:
        power = nn(split(gram[...]), split(basis[...]))
        total = jnp.sum(power * power, keepdims=True)
        out[...] = power / (jnp.sqrt(total) + 1e-06)

    def refresh(step, carry):
        pieces = [split(out[...]) for _, _, out in sides]
        outer = [nt(p, p) for p in pieces]
        for p, w, (_, _, out) in zip(pieces, outer, sides):
            out[...] = 1.5 * out[...] - 0.5 * nn(split(w), p)
        return carry

    lax.fori_loop(0, 2, refresh, 0)

    for k in order:
        landing(part, sum_send_sem, sum_recv_sem, shard_peer(k)).wait_recv()
    column = part[0]
    for i in range(1, shards):
        column = column + part[i]
    part_all[col] = column
    all_copies = [all_copy(k) for k in range(1, tensors)]
    for copy in all_copies:
        copy.start()

    lax.fori_loop(2, 3, refresh, 0)

    for copy in loads[5:]:
        copy.wait()
    right = split(right_v[...])
    arriving = [me] + [lax.rem(me + shards - k, shards) for k in order]
    parties = (arriving[:4], arriving[4:])
    turned = [split(left_rows(party).T) for party in parties]
    level = jnp.clip(jnp.sqrt(jnp.sum(column, keepdims=True)), F32(1.0), F32(1e30))
    rotated_unit = None
    for party, side in zip(parties, turned):
        for source in party:
            if source is not me:
                landing(grad_block, grad_send_sem, grad_recv_sem, source).wait_recv()
        rows = jnp.concatenate([grad_block[source] for source in party], axis=0)
        term = nn(side, split(nn(split(rows * (1.0 / level)), right)))
        rotated_unit = term if rotated_unit is None else rotated_unit + term

    for k in range(1, tensors):
        source = lax.rem(col + tensors - k, tensors)
        pltpu.make_async_remote_copy(
            src_ref=part_all.at[source], dst_ref=part_all.at[source],
            send_sem=all_send_sem.at[k - 1], recv_sem=all_recv_sem.at[k - 1],
            device_id=(me, tensor_peer(k)), device_id_type=MESH,
        ).wait_recv()
    whole = part_all[0]
    for i in range(1, tensors):
        whole = whole + part_all[i]
    total = jnp.sum(whole, keepdims=True)
    scale = level * jnp.minimum(F32(1.0), F32(limit) / (jnp.sqrt(total) + 1e-06))

    rotated = scale * rotated_unit
    moment_new = 0.9 * moment_v[...] + 0.1 * rotated
    second_new = 0.95 * second_v[...] + 0.05 * rotated * rotated
    moment_out[...] = moment_new
    second_out[...] = second_new
    normalized = moment_new / (jnp.sqrt(second_new) + 1e-08)
    half_done = split(nt(split(normalized), right))
    up_copies = [up_copy(p) for p in update_peers]
    for copies, party in (
        (up_copies[:3], update_peers[:3]), (up_copies[3:], update_peers[3:] + [me]),
    ):
        update = nn(split(left_rows(party)), half_done)
        for i, target in enumerate(party):
            update_send[target] = update[i * rows_piece:(i + 1) * rows_piece]
        for copy in copies:
            copy.start()

    unit = grad_block[...].reshape(block, block) * (1.0 / level)
    g = split(unit)
    left_gram_out[...] = 0.9 * left_gram_v[...] + (0.1 * scale * scale) * nt(g, g)
    right_gram_out[...] = 0.9 * right_gram_v[...] + (0.1 * scale * scale) * nn(split(unit.T), g)

    lax.fori_loop(3, NS_ITERS, refresh, 0)

    def finish(at, update):
        old = weights_v[at]
        weights_out[at] = old - learn_rate * (update + weight_decay * old)

    finish(me, update_send[me])
    for k in order:
        source = shard_peer(k)
        landing(update_recv, up_send_sem, up_recv_sem, source).wait_recv()
        finish(source, update_recv[source])
    for copy in sum_copies + grad_copies + all_copies + up_copies:
        copy.wait_send()


def put_kernel(*refs):
    count = (len(refs) - 1) // 2
    sem = refs[-1]
    copies = [pltpu.make_async_copy(refs[i], refs[count + i], sem.at[i]) for i in range(count)]
    for copy in copies:
        copy.start()
    for copy in copies:
        copy.wait()


def local_kernel(grad, weights, moment, second, left_basis, right_basis, left_gram, right_gram):
    shards = lax.axis_size("shard")
    tensors = lax.axis_size("tensor")
    block = left_basis.shape[-1]
    rows_piece = block // shards
    train_shape = grad.shape
    limit = 0.5 * float(block * block * shards * tensors) ** 0.5
    pieces = (shards, rows_piece, block)
    square = (block, block)
    shapes = (pieces,) + (square,) * 6
    results = pl.pallas_call(
        functools.partial(step_kernel, shards, tensors, limit),
        out_shape=[pltpu.VMEM(s, F32) for s in shapes],
        in_specs=[pl.BlockSpec(memory_space=pl.ANY)] * 8,
        out_specs=[pl.BlockSpec(memory_space=pltpu.VMEM)] * 7,
        scratch_shapes=[
            pltpu.VMEM(pieces, F32),
            pltpu.VMEM(pieces, F32),
        ] + [pltpu.VMEM(square, F32)] * 6 + [pltpu.VMEM(pieces, F32)] * 3 + [
            pltpu.VMEM((shards, 1, 128), F32),
            pltpu.VMEM((tensors, 1, 128), F32),
            pltpu.SemaphoreType.DMA((8,)),
        ] + [pltpu.SemaphoreType.DMA((shards,))] * 6
        + [pltpu.SemaphoreType.DMA((tensors - 1,))] * 2,
        compiler_params=pltpu.CompilerParams(collective_id=0, has_side_effects=True),
        name="soap_step",
    )(
        grad.reshape(pieces), weights.reshape(pieces),
        *(a.reshape(square) for a in (moment, second, left_basis, right_basis, left_gram, right_gram)),
    )
    outs = pl.pallas_call(
        put_kernel,
        out_shape=[jax.ShapeDtypeStruct(s, F32) for s in shapes],
        in_specs=[pl.BlockSpec(memory_space=pltpu.VMEM)] * 7,
        out_specs=[pl.BlockSpec(memory_space=pl.ANY)] * 7,
        scratch_shapes=[pltpu.SemaphoreType.DMA((7,))],
        name="put_out",
    )(*(pltpu.with_memory_space_constraint(r, pltpu.VMEM) for r in results))
    return (outs[0].reshape(train_shape),) + tuple(o[None, None] for o in outs[1:])


def matmul_nn(left, right):
    return jnp.dot(left, right, precision=lax.Precision.HIGHEST, preferred_element_type=F32)


def matmul_tn(left, right):
    return lax.dot_general(
        left, right, (((0,), (0,)), ((), ())),
        precision=lax.Precision.HIGHEST, preferred_element_type=F32,
    )


def matmul_nt(left, right):
    return lax.dot_general(
        left, right, (((1,), (1,)), ((), ())),
        precision=lax.Precision.HIGHEST, preferred_element_type=F32,
    )


def refresh_plain(gram, basis):
    power = matmul_nn(gram, basis)
    iterate = power / (jnp.sqrt(jnp.sum(power * power)) + 1e-06)
    for step in range(NS_ITERS):
        iterate = 1.5 * iterate - 0.5 * matmul_nn(iterate, matmul_tn(iterate, iterate))
    return iterate


def local_plain(grad, weights, moment, second, left_basis, right_basis, left_gram, right_gram):
    shards = lax.axis_size("shard")
    devices = shards * lax.axis_size("tensor")
    block = left_basis.shape[-1]
    pieces = (shards, block // shards, block)
    left_now = left_basis[0, 0]
    right_now = right_basis[0, 0]
    left_stat = left_gram[0, 0]
    right_stat = right_gram[0, 0]
    squares = lax.psum(jnp.sum(grad * grad), ("shard", "tensor"))
    received = lax.all_to_all(grad.reshape(pieces), "shard", split_axis=0, concat_axis=0, tiled=True)
    limit = 0.5 * jnp.sqrt(F32(block * block * devices))
    scale = jnp.minimum(F32(1.0), limit / (jnp.sqrt(squares) + 1e-06))
    scaled = scale * received.reshape(block, block)
    rotated = matmul_tn(left_now, matmul_nn(scaled, right_now))
    moment_new = 0.9 * moment[0, 0] + 0.1 * rotated
    second_new = 0.95 * second[0, 0] + 0.05 * rotated * rotated
    normalized = moment_new / (jnp.sqrt(second_new) + 1e-08)
    update = matmul_nt(matmul_nn(left_now, normalized), right_now)
    returned = lax.all_to_all(update.reshape(pieces), "shard", split_axis=0, concat_axis=0, tiled=True)
    new_weights = weights - learn_rate * (returned.reshape(grad.shape) + weight_decay * weights)
    rest = (
        moment_new,
        second_new,
        refresh_plain(left_stat, left_now),
        refresh_plain(right_stat, right_now),
        0.9 * left_stat + 0.1 * matmul_nt(scaled, scaled),
        0.9 * right_stat + 0.1 * matmul_tn(scaled, scaled),
    )
    return (new_weights,) + tuple(r[None, None] for r in rest)


def local(grad, *rest):
    shards = lax.axis_size("shard")
    fits = shards == len(GRAD_ORDER) and rest[1].shape[-1] // shards % 8 == 0
    run = local_kernel if fits else local_plain
    return run(grad, *rest)


def solution(mesh):
    train = P(None, "shard", "tensor")
    owned = P("tensor", "shard", None, None)
    return jax.shard_map(
        local, mesh=mesh, in_specs=(train, train) + (owned,) * 6,
        out_specs=(train,) + (owned,) * 6, check_vma=False,
    )
```

```python
import functools

import jax
import jax.numpy as jnp
from jax import lax
from jax.experimental import pallas as pl
from jax.experimental.pallas import tpu as pltpu
from jax.sharding import PartitionSpec as P

NS_ITERS = 5


learn_rate = 0.03
weight_decay = 0.1

MESH = pl.DeviceIdType.MESH
F32 = jnp.float32
BF16 = jnp.bfloat16


def split(x):
    hi = x.astype(BF16)
    lo = (x - hi.astype(F32)).astype(BF16)
    return hi, lo


def nn(a, b):
    left = jnp.concatenate([a[0], a[1], a[0]], axis=1)
    right = jnp.concatenate([b[0], b[0], b[1]], axis=0)
    return jnp.dot(left, right, preferred_element_type=F32)


def nt(a, b):
    left = jnp.concatenate([a[0], a[1], a[0]], axis=1)
    right = jnp.concatenate([b[0], b[0], b[1]], axis=1)
    return lax.dot_general(left, right, (((1,), (1,)), ((), ())), preferred_element_type=F32)


GRAD_ORDER = (
    (1, 2, 3, 4, 5, 6, 7),
    (2, 3, 4, 5, 6, 7, 0),
    (3, 4, 5, 6, 7, 0, 1),
    (4, 5, 6, 7, 0, 1, 2),
    (5, 6, 7, 0, 1, 2, 3),
    (6, 7, 0, 1, 2, 3, 4),
    (7, 0, 1, 2, 3, 4, 5),
    (0, 1, 2, 3, 4, 5, 6),
)
UPDATE_ORDER = (
    (1, 2, 3, 4, 5, 6, 7),
    (0, 2, 3, 4, 5, 6, 7),
    (0, 1, 3, 4, 5, 6, 7),
    (0, 1, 2, 4, 5, 6, 7),
    (0, 1, 2, 3, 5, 6, 7),
    (0, 1, 2, 3, 4, 6, 7),
    (0, 1, 2, 3, 4, 5, 7),
    (0, 1, 2, 3, 4, 5, 6),
)

SUM_ORDER = (
    (7, 6, 5, 4, 3, 2, 1),
    (7, 6, 5, 4, 3, 2, 0),
    (7, 6, 5, 4, 3, 1, 0),
    (7, 6, 5, 4, 2, 1, 0),
    (0, 1, 2, 3, 5, 6, 7),
    (0, 1, 2, 3, 4, 6, 7),
    (0, 1, 2, 3, 4, 5, 7),
    (0, 1, 2, 3, 4, 5, 6),
)

def peer_table(order, me):
    bit0, bit1, bit2 = lax.rem(me, 2), lax.rem(lax.div(me, 2), 2), lax.div(me, 4)
    place = (1 + 7 * bit0) * (1 + 63 * bit1) * (1 + 4095 * bit2)
    packed = [sum(row[j] * 8 ** i for i, row in enumerate(order)) for j in range(len(order) - 1)]
    return [lax.rem(lax.div(jnp.int32(p), place), 8) for p in packed]


def step_kernel(
    shards, tensors, limit,
    grad, weights, moment, second, left_basis, right_basis, left_gram, right_gram,
    weights_out, moment_out, second_out, left_out, right_out, left_gram_out, right_gram_out,
    grad_own, weights_v, moment_v, second_v, left_v, right_v, left_gram_v, right_gram_v,
    grad_block, update_send, update_recv, part, part_all,
    load_sem, grad_send_sem, grad_recv_sem, up_send_sem, up_recv_sem,
    sum_send_sem, sum_recv_sem, all_send_sem, all_recv_sem,
):
    block = left_v.shape[-1]
    me = lax.axis_index("shard")
    col = lax.axis_index("tensor")
    order = list(range(1, shards))
    grad_peers = peer_table(GRAD_ORDER, me)
    update_peers = peer_table(UPDATE_ORDER, me)

    rows_piece = block // shards

    def left_rows(party):
        starts = [pl.multiple_of(i * rows_piece, rows_piece) for i in party]
        return jnp.concatenate([left_v[pl.ds(start, rows_piece), :] for start in starts], axis=0)

    def shard_peer(k):
        return lax.rem(me + k, shards)

    def tensor_peer(k):
        return lax.rem(col + k, tensors)

    barrier = pltpu.get_barrier_semaphore()
    for k in order:
        pl.semaphore_signal(barrier, inc=1, device_id=(shard_peer(k), col), device_id_type=MESH)
    for k in range(1, tensors):
        pl.semaphore_signal(barrier, inc=1, device_id=(me, tensor_peer(k)), device_id_type=MESH)

    loads = [
        pltpu.make_async_copy(src, dst, load_sem.at[i])
        for i, (src, dst) in enumerate((
            (grad, grad_own),
            (left_gram, left_gram_v),
            (left_basis, left_v),
            (right_gram, right_gram_v),
            (right_basis, right_v),
            (moment, moment_v),
            (second, second_v),
            (weights, weights_v),
        ))
    ]
    for copy in loads:
        copy.start()

    loads[0].wait()
    own = grad_own[...].reshape(block, block)
    squares = jnp.sum((own * own).reshape(block // 8, 8, block), axis=0)
    tile = squares[:, :128]
    for start in range(128, block, 128):
        tile = tile + squares[:, start:start + 128]
    tile = jnp.sum(tile, axis=0, keepdims=True)
    part[me] = tile

    pl.semaphore_wait(barrier, shards - 1 + tensors - 1)

    def grad_copy(peer):
        return pltpu.make_async_remote_copy(
            src_ref=grad_own.at[peer], dst_ref=grad_block.at[me],
            send_sem=grad_send_sem.at[peer], recv_sem=grad_recv_sem.at[me],
            device_id=(peer, col), device_id_type=MESH,
        )

    def sum_copy(peer):
        return pltpu.make_async_remote_copy(
            src_ref=part.at[me], dst_ref=part.at[me],
            send_sem=sum_send_sem.at[peer], recv_sem=sum_recv_sem.at[me],
            device_id=(peer, col), device_id_type=MESH,
        )

    def all_copy(k):
        return pltpu.make_async_remote_copy(
            src_ref=part_all.at[col], dst_ref=part_all.at[col],
            send_sem=all_send_sem.at[k - 1], recv_sem=all_recv_sem.at[k - 1],
            device_id=(me, tensor_peer(k)), device_id_type=MESH,
        )

    def up_copy(peer):
        return pltpu.make_async_remote_copy(
            src_ref=update_send.at[peer], dst_ref=update_recv.at[me],
            send_sem=up_send_sem.at[peer], recv_sem=up_recv_sem.at[me],
            device_id=(peer, col), device_id_type=MESH,
        )

    def landing(buffer, send, recv, source):
        return pltpu.make_async_remote_copy(
            src_ref=buffer.at[source], dst_ref=buffer.at[source],
            send_sem=send.at[source], recv_sem=recv.at[source],
            device_id=(source, col), device_id_type=MESH,
        )

    sum_copies = [sum_copy(p) for p in peer_table(SUM_ORDER, me)]
    grad_copies = [grad_copy(p) for p in grad_peers]
    for copy in sum_copies:
        copy.start()
    for copy in grad_copies:
        copy.start()
    grad_block[me] = grad_own[me]

    for copy in loads[1:5]:
        copy.wait()
    sides = ((left_gram_v, left_v, left_out), (right_gram_v, right_v, right_out))
    for gram, basis, out in sides:
        power = nn(split(gram[...]), split(basis[...]))
        total = jnp.sum(power * power, keepdims=True)
        out[...] = power / (jnp.sqrt(total) + 1e-06)

    def refresh(step, carry):
        pieces = [split(out[...]) for _, _, out in sides]
        outer = [nt(p, p) for p in pieces]
        for p, w, (_, _, out) in zip(pieces, outer, sides):
            out[...] = 1.5 * out[...] - 0.5 * nn(split(w), p)
        return carry

    lax.fori_loop(0, 2, refresh, 0)

    for k in order:
        landing(part, sum_send_sem, sum_recv_sem, shard_peer(k)).wait_recv()
    column = part[0]
    for i in range(1, shards):
        column = column + part[i]
    part_all[col] = column
    all_copies = [all_copy(k) for k in (2, 1, 3)]
    for copy in all_copies:
        copy.start()

    lax.fori_loop(2, 3, refresh, 0)

    for copy in loads[5:]:
        copy.wait()
    right = split(right_v[...])
    arriving = [me] + [lax.rem(me + shards - k, shards) for k in order]
    parties = (arriving[:4], arriving[4:])
    turned = [split(left_rows(party).T) for party in parties]
    level = jnp.clip(jnp.sqrt(jnp.sum(column, keepdims=True)), F32(1.0), F32(1e30))
    rotated_unit = None
    for party, side in zip(parties, turned):
        for source in party:
            if source is not me:
                landing(grad_block, grad_send_sem, grad_recv_sem, source).wait_recv()
        rows = jnp.concatenate([grad_block[source] for source in party], axis=0)
        term = nn(side, split(nn(split(rows * (1.0 / level)), right)))
        rotated_unit = term if rotated_unit is None else rotated_unit + term

    for k in range(1, tensors):
        source = lax.rem(col + tensors - k, tensors)
        pltpu.make_async_remote_copy(
            src_ref=part_all.at[source], dst_ref=part_all.at[source],
            send_sem=all_send_sem.at[k - 1], recv_sem=all_recv_sem.at[k - 1],
            device_id=(me, tensor_peer(k)), device_id_type=MESH,
        ).wait_recv()
    whole = part_all[0]
    for i in range(1, tensors):
        whole = whole + part_all[i]
    total = jnp.sum(whole, keepdims=True)
    scale = level * jnp.minimum(F32(1.0), F32(limit) / (jnp.sqrt(total) + 1e-06))

    rotated = scale * rotated_unit
    moment_new = 0.9 * moment_v[...] + 0.1 * rotated
    second_new = 0.95 * second_v[...] + 0.05 * rotated * rotated
    moment_out[...] = moment_new
    second_out[...] = second_new
    normalized = moment_new / (jnp.sqrt(second_new) + 1e-08)
    half_done = split(nt(split(normalized), right))
    up_copies = [up_copy(p) for p in update_peers]
    for copies, party in (
        (up_copies[:3], update_peers[:3]), (up_copies[3:], update_peers[3:] + [me]),
    ):
        update = nn(split(left_rows(party)), half_done)
        for i, target in enumerate(party):
            update_send[target] = update[i * rows_piece:(i + 1) * rows_piece]
        for copy in copies:
            copy.start()

    unit = grad_block[...].reshape(block, block) * (1.0 / level)
    g = split(unit)
    left_gram_out[...] = 0.9 * left_gram_v[...] + (0.1 * scale * scale) * nt(g, g)
    right_gram_out[...] = 0.9 * right_gram_v[...] + (0.1 * scale * scale) * nn(split(unit.T), g)

    lax.fori_loop(3, NS_ITERS, refresh, 0)

    def finish(at, update):
        old = weights_v[at]
        weights_out[at] = old - learn_rate * (update + weight_decay * old)

    finish(me, update_send[me])
    for k in order:
        source = shard_peer(k)
        landing(update_recv, up_send_sem, up_recv_sem, source).wait_recv()
        finish(source, update_recv[source])
    for copy in sum_copies + grad_copies + all_copies + up_copies:
        copy.wait_send()


def put_kernel(*refs):
    count = (len(refs) - 1) // 2
    sem = refs[-1]
    copies = [pltpu.make_async_copy(refs[i], refs[count + i], sem.at[i]) for i in range(count)]
    for copy in copies:
        copy.start()
    for copy in copies:
        copy.wait()


def local_kernel(grad, weights, moment, second, left_basis, right_basis, left_gram, right_gram):
    shards = lax.axis_size("shard")
    tensors = lax.axis_size("tensor")
    block = left_basis.shape[-1]
    rows_piece = block // shards
    train_shape = grad.shape
    limit = 0.5 * float(block * block * shards * tensors) ** 0.5
    pieces = (shards, rows_piece, block)
    square = (block, block)
    shapes = (pieces,) + (square,) * 6
    results = pl.pallas_call(
        functools.partial(step_kernel, shards, tensors, limit),
        out_shape=[pltpu.VMEM(s, F32) for s in shapes],
        in_specs=[pl.BlockSpec(memory_space=pl.ANY)] * 8,
        out_specs=[pl.BlockSpec(memory_space=pltpu.VMEM)] * 7,
        scratch_shapes=[
            pltpu.VMEM(pieces, F32),
            pltpu.VMEM(pieces, F32),
        ] + [pltpu.VMEM(square, F32)] * 6 + [pltpu.VMEM(pieces, F32)] * 3 + [
            pltpu.VMEM((shards, 1, 128), F32),
            pltpu.VMEM((tensors, 1, 128), F32),
            pltpu.SemaphoreType.DMA((8,)),
        ] + [pltpu.SemaphoreType.DMA((shards,))] * 6
        + [pltpu.SemaphoreType.DMA((tensors - 1,))] * 2,
        compiler_params=pltpu.CompilerParams(collective_id=0, has_side_effects=True),
        name="soap_step",
    )(
        grad.reshape(pieces), weights.reshape(pieces),
        *(a.reshape(square) for a in (moment, second, left_basis, right_basis, left_gram, right_gram)),
    )
    outs = pl.pallas_call(
        put_kernel,
        out_shape=[jax.ShapeDtypeStruct(s, F32) for s in shapes],
        in_specs=[pl.BlockSpec(memory_space=pltpu.VMEM)] * 7,
        out_specs=[pl.BlockSpec(memory_space=pl.ANY)] * 7,
        scratch_shapes=[pltpu.SemaphoreType.DMA((7,))],
        name="put_out",
    )(*(pltpu.with_memory_space_constraint(r, pltpu.VMEM) for r in results))
    return (outs[0].reshape(train_shape),) + tuple(o[None, None] for o in outs[1:])


def matmul_nn(left, right):
    return jnp.dot(left, right, precision=lax.Precision.HIGHEST, preferred_element_type=F32)


def matmul_tn(left, right):
    return lax.dot_general(
        left, right, (((0,), (0,)), ((), ())),
        precision=lax.Precision.HIGHEST, preferred_element_type=F32,
    )


def matmul_nt(left, right):
    return lax.dot_general(
        left, right, (((1,), (1,)), ((), ())),
        precision=lax.Precision.HIGHEST, preferred_element_type=F32,
    )


def refresh_plain(gram, basis):
    power = matmul_nn(gram, basis)
    iterate = power / (jnp.sqrt(jnp.sum(power * power)) + 1e-06)
    for step in range(NS_ITERS):
        iterate = 1.5 * iterate - 0.5 * matmul_nn(iterate, matmul_tn(iterate, iterate))
    return iterate


def local_plain(grad, weights, moment, second, left_basis, right_basis, left_gram, right_gram):
    shards = lax.axis_size("shard")
    devices = shards * lax.axis_size("tensor")
    block = left_basis.shape[-1]
    pieces = (shards, block // shards, block)
    left_now = left_basis[0, 0]
    right_now = right_basis[0, 0]
    left_stat = left_gram[0, 0]
    right_stat = right_gram[0, 0]
    squares = lax.psum(jnp.sum(grad * grad), ("shard", "tensor"))
    received = lax.all_to_all(grad.reshape(pieces), "shard", split_axis=0, concat_axis=0, tiled=True)
    limit = 0.5 * jnp.sqrt(F32(block * block * devices))
    scale = jnp.minimum(F32(1.0), limit / (jnp.sqrt(squares) + 1e-06))
    scaled = scale * received.reshape(block, block)
    rotated = matmul_tn(left_now, matmul_nn(scaled, right_now))
    moment_new = 0.9 * moment[0, 0] + 0.1 * rotated
    second_new = 0.95 * second[0, 0] + 0.05 * rotated * rotated
    normalized = moment_new / (jnp.sqrt(second_new) + 1e-08)
    update = matmul_nt(matmul_nn(left_now, normalized), right_now)
    returned = lax.all_to_all(update.reshape(pieces), "shard", split_axis=0, concat_axis=0, tiled=True)
    new_weights = weights - learn_rate * (returned.reshape(grad.shape) + weight_decay * weights)
    rest = (
        moment_new,
        second_new,
        refresh_plain(left_stat, left_now),
        refresh_plain(right_stat, right_now),
        0.9 * left_stat + 0.1 * matmul_nt(scaled, scaled),
        0.9 * right_stat + 0.1 * matmul_tn(scaled, scaled),
    )
    return (new_weights,) + tuple(r[None, None] for r in rest)


def local(grad, *rest):
    shards = lax.axis_size("shard")
    fits = shards == len(GRAD_ORDER) and rest[1].shape[-1] // shards % 8 == 0
    run = local_kernel if fits else local_plain
    return run(grad, *rest)


def solution(mesh):
    train = P(None, "shard", "tensor")
    owned = P("tensor", "shard", None, None)
    return jax.shard_map(
        local, mesh=mesh, in_specs=(train, train) + (owned,) * 6,
        out_specs=(train,) + (owned,) * 6, check_vma=False,
    )
```
